32 devices in a mesh: grp: 2 (over x), band: 16 (over z, y, core).
Axes of the slice: x: 2, y: 2, z: 4, core: 2. Of those that a mesh axis runs over, the one named last changes fastest.
Arguments:
- samples: float32 [2, 192, 8192], P(None, None, ('grp', 'band')), parts along dimension 2, may hold values from -6 to 6
- prototype: float32 [16, 128], replicated, may hold values from -1.5 to 1.5
- dish_filter: float32 [2, 8, 192, 128], replicated, may hold values from -1.5 to 1.5
- beam_weights: float32 [16, 8, 2, 192, 192], P('band'), may hold values from -0.3125 to 0.3125
- dish_order: int32 [192], replicated, may hold values from 0 to 191, each once
Outputs:
- power: float32 [32, 8, 192, 8], P(('grp', 'band')), parts along dimension 0
The draws below stay inside these ranges and needn't reach their ends.
There are 2 independent parts, one for each index of `grp`. The reference program is written for one: setup_inputs(seed, part) draws one part's arguments, and reference() takes and returns one part's arrays. A program takes and returns all parts, laid end to end along the dimension named above; an argument that names none is the same for every part. Nothing has to cross between parts.
Inputs may be any that keep to these rules, and one draw needn't show every extreme that they name: `dish_order`: each of the 192 dishes stands in exactly one panel slot.
All inputs are finite; a program needn't handle non-finite values.
Results may differ from the reference program's by a relative error of at most 0.0003.
Values sent between devices are 32-bit elements; how exact they have to be, the bound alone decides.
A program may use at most 64 MiB of HBM per device.

```python
import math
import jax
import jax.numpy as jnp
from jax import lax

DISHES = 192
CHAN = 128
BANDW = 8
PFB_TAPS = 16
FIR_TAPS = 8
BEAM_DEV = 192
INTEG = 4
OWNERS = 1
FRAMES = 32
SAMPLES = 4096
N_BAND = 16


def steps_of(rng, extent, split, smallest, largest):
    factor_of, own = 1.0, jax.random.fold_in(rng, 6)
    for dim, blocks in split:
        steps = jnp.exp(jax.random.uniform(jax.random.fold_in(own, dim), (blocks,), jnp.float32, smallest / len(split), largest / len(split)))
        factor_of = factor_of * jnp.repeat(steps, extent[dim] // blocks).reshape([-1 if axis == dim else 1 for axis in range(len(extent))])
    return factor_of


def bell_draw(key, shape, width, bound, cuts=(), kind=jnp.bfloat16):
    values = jax.random.normal(key, shape, jnp.float32) * width
    if len(cuts) > 0:
        values = steps_of(key, shape, cuts, -0.22, 0.18) * values
    return jnp.clip(values, min=-bound, max=bound).astype(kind)


def setup_inputs(seed: int = 0, part: int = 0) -> dict:
    streams_of = jax.random.split(jax.random.key(seed), 6)
    part_splits = jax.random.split(jax.random.fold_in(streams_of[5], part), 6)
    samples = bell_draw(part_splits[0], (2, DISHES, SAMPLES), 1.0, 6.0, ((2, 16),), jnp.float32)
    prototype = bell_draw(streams_of[1], (PFB_TAPS, CHAN), 0.25, 1.5, (), jnp.float32)
    dish_filter = bell_draw(streams_of[2], (2, FIR_TAPS, DISHES, CHAN), 0.25, 1.5, (), jnp.float32)
    beam_weights = bell_draw(streams_of[3], (N_BAND, BANDW, 2, DISHES, BEAM_DEV), (2 * DISHES) ** -0.5, 0.3125, ((0, 16),), jnp.float32)
    dish_order = jax.random.permutation(streams_of[4], DISHES).astype(jnp.int32)
    return dict(samples=samples, prototype=prototype, dish_filter=dish_filter, beam_weights=beam_weights, dish_order=dish_order)


def fourier_tables(length):
    counter = jnp.arange(length, dtype=jnp.int32)
    product = counter[:, None] * counter[None, :] % length
    angles = product.astype(jnp.float32) * (2.0 * math.pi / length)
    factor = 1.0 / math.sqrt(length)
    return (jnp.cos(angles) * factor, jnp.sin(angles) * factor)

def filter_frames(real_in, imag_in, tap_real, tap_imag, frame_count):
    tap_count = tap_real.shape[0]
    out_real = jnp.zeros(real_in.shape[:-1] + (frame_count,), real_in.dtype)
    out_imag = jnp.zeros(real_in.shape[:-1] + (frame_count,), real_in.dtype)
    for tap_index in range(tap_count):
        offset = tap_count - 1 - tap_index
        part_real = real_in[..., offset:offset + frame_count]
        part_imag = imag_in[..., offset:offset + frame_count]
        factor_real = tap_real[tap_index][..., None]
        factor_imag = tap_imag[tap_index][..., None]
        out_real = out_real + factor_real * part_real - factor_imag * part_imag
        out_imag = out_imag + factor_real * part_imag + factor_imag * part_real
    return (out_real, out_imag)

def detect(weights, field_real, field_imag):
    highest = lax.Precision.HIGHEST

    def contract(weight_part, field_part):
        return jnp.einsum('qds,dqf->qsf', weight_part, field_part, precision=highest)
    beam_real = contract(weights[:, 0], field_real) - contract(weights[:, 1], field_imag)
    beam_imag = contract(weights[:, 0], field_imag) + contract(weights[:, 1], field_real)
    energy = beam_real * beam_real + beam_imag * beam_imag
    shaped = energy.reshape(energy.shape[:-1] + (energy.shape[-1] // INTEG, INTEG))
    return lax.optimization_barrier(jnp.mean(shaped, axis=-1))

def reference(samples, prototype, dish_filter, beam_weights, dish_order):
    highest = lax.Precision.HIGHEST
    ordered = samples[:, dish_order, :]
    blocks = ordered.reshape(2, DISHES, FRAMES, CHAN)
    padded = jnp.pad(blocks, ((0, 0), (0, 0), (PFB_TAPS - 1, 0), (0, 0)))
    polyphase = jnp.zeros_like(blocks)
    for tap_index in range(PFB_TAPS):
        offset = PFB_TAPS - 1 - tap_index
        polyphase = polyphase + prototype[tap_index] * padded[:, :, offset:offset + FRAMES, :]
    cosine_table, sine_table = fourier_tables(CHAN)
    spec_real = jnp.dot(polyphase[0], cosine_table, precision=highest) + jnp.dot(polyphase[1], sine_table, precision=highest)
    spec_imag = jnp.dot(polyphase[1], cosine_table, precision=highest) - jnp.dot(polyphase[0], sine_table, precision=highest)
    spec_real = jnp.transpose(spec_real, (0, 2, 1))
    spec_imag = jnp.transpose(spec_imag, (0, 2, 1))
    widths = ((0, 0), (0, 0), (FIR_TAPS - 1, 0))
    taps_ordered = dish_filter[:, :, dish_order, :]
    filtered_real, filtered_imag = filter_frames(jnp.pad(spec_real, widths), jnp.pad(spec_imag, widths), taps_ordered[0], taps_ordered[1], FRAMES)

    def one_row(row_item):
        row_index, weights = row_item
        first_chan = row_index // OWNERS * BANDW
        band_real = lax.dynamic_slice_in_dim(filtered_real, first_chan, BANDW, 1)
        band_imag = lax.dynamic_slice_in_dim(filtered_imag, first_chan, BANDW, 1)
        return detect(weights, band_real, band_imag)
    return lax.map(one_row, (jnp.arange(N_BAND, dtype=jnp.int32), beam_weights))
```

```python
import functools
import math

import jax
import jax.numpy as jnp
import ml_dtypes
import numpy as np
from jax import lax
from jax.experimental import pallas as pl
from jax.experimental.pallas import tpu as pltpu
from jax.sharding import PartitionSpec as P

INTEG = 4
CHUNK = 32
F32 = jnp.float32
BF16 = jnp.bfloat16


def split(value):
    high = value.astype(BF16)
    return high, (value - high.astype(F32)).astype(BF16)


def dot(lhs, rhs):
    return jnp.dot(lhs, rhs, preferred_element_type=F32)


def dot3(lhs, rhs):
    return dot(lhs[0], rhs[0]) + (dot(lhs[0], rhs[1]) + dot(lhs[1], rhs[0]))


def fourier_matrix(length):
    counter = np.arange(length)
    angles = (counter[:, None] * counter[None, :] % length) * (2.0 * math.pi / length)
    cosine = np.cos(angles) / math.sqrt(length)
    sine = np.sin(angles) / math.sqrt(length)
    full = np.block([[cosine, -sine], [sine, cosine]]).astype(np.float32)
    high = full.astype(ml_dtypes.bfloat16)
    low = (full - high.astype(np.float32)).astype(ml_dtypes.bfloat16)
    return np.stack([high, low])


def kernel(
    dims,
    x_ref,
    proto_ref,
    order_ref,
    fourier_hbm,
    taps_hbm,
    weights_hbm,
    out_ref,
    stage,
    voltages,
    spectra,
    filtered,
    turned,
    panels,
    fourier,
    taps,
    weights,
    beams_high,
    beams_low,
    load_sems,
    sems,
):
    devices, workers, group, slice_frames, frames, owners = dims
    pfb = proto_ref.shape[0]
    chan = proto_ref.shape[1]
    fir = taps.shape[1]
    dishes = order_ref.shape[1]
    band_chans, _, _, beams = weights.shape
    pairs = group // 2
    chunks = frames // CHUNK
    half = workers * pairs
    me = lax.axis_index("band")
    worker = (me * workers + devices - 1) // devices
    active = jnp.logical_and(worker < workers, worker * devices // workers == me)
    worker = jnp.minimum(worker, workers - 1)
    dish_start = pl.multiple_of(worker * group, group)

    load_weights = pltpu.make_async_copy(weights_hbm.at[0], weights, load_sems.at[0])
    load_taps = pltpu.make_async_copy(
        taps_hbm.at[:, :, pl.ds(dish_start, group), :], taps, load_sems.at[1]
    )
    load_fourier = pltpu.make_async_copy(fourier_hbm, fourier, load_sems.at[2])

    barrier = pltpu.get_barrier_semaphore()

    @pl.loop(1, devices)
    def _(step):
        pl.semaphore_signal(barrier, inc=1, device_id={"band": lax.rem(me + step, devices)})

    load_weights.start()
    load_taps.start()
    load_fourier.start()
    for target in range(workers):
        for frame in range(slice_frames):
            for part in range(2):
                stage[target, frame, part] = x_ref[
                    part,
                    target * group : (target + 1) * group,
                    frame * chan : (frame + 1) * chan,
                ]
    pl.semaphore_wait(barrier, devices - 1)

    arrival = pl.ds(pfb - 1 + me * slice_frames, slice_frames)

    @pl.loop(0, workers)
    def _(step):
        target = lax.rem(worker + step, workers)
        device = target * devices // workers

        @pl.when(device != me)
        def _():
            pltpu.make_async_remote_copy(
                src_ref=stage.at[target],
                dst_ref=voltages.at[arrival],
                send_sem=sems.at[0],
                recv_sem=sems.at[1],
                device_id={"band": device},
            ).start()

        @pl.when(device == me)
        def _():
            pltpu.make_async_copy(stage.at[target], voltages.at[arrival], sems.at[1]).start()

    row = lax.broadcasted_iota(jnp.int32, (dishes, dishes), 0)
    dish_of_row = jnp.where(row < half, 2 * row, 2 * (row - half) + 1)
    chosen = jnp.where(order_ref[...] == dish_of_row, 1.0, 0.0).astype(BF16)
    load_weights.wait()

    @pl.loop(0, band_chans)
    def _(index):
        for part in range(2):
            high, low = split(weights[index, part])
            rows = slice(part * beams, (part + 1) * beams)
            beams_high[index, rows, :] = dot(chosen, high).T.astype(BF16)
            beams_low[index, rows, :] = dot(chosen, low).T.astype(BF16)

    load_taps.wait()
    load_fourier.wait()

    @pl.when(active)
    def _():
        voltages[0 : pfb - 1] = jnp.zeros((pfb - 1, 2, group, chan), F32)
        spectra[:, 0 : fir - 1] = jnp.zeros((2, fir - 1, group, chan), F32)
        landed = voltages.at[pl.ds(pfb - 1, frames)]
        pltpu.make_async_copy(landed, landed, sems.at[1]).wait()
        step_frames = 8

        @pl.loop(0, frames // step_frames)
        def _(step):
            first = step * step_frames
            pieces = []
            for part in range(2):
                total = jnp.zeros((step_frames, group, chan), F32)
                for tap in range(pfb):
                    total = total + proto_ref[tap : tap + 1, :] * voltages[
                        pl.ds(first + pfb - 1 - tap, step_frames), part
                    ]
                pieces.append(total.reshape(step_frames * group, chan))
            lhs = split(jnp.concatenate(pieces, axis=1))
            result = dot3(lhs, (fourier[0], fourier[1]))
            for part in range(2):
                spectra[part, pl.ds(first + fir - 1, step_frames)] = result[
                    :, part * chan : (part + 1) * chan
                ].reshape(step_frames, group, chan)

        @pl.loop(0, frames // step_frames)
        def _(step):
            first = step * step_frames
            out_real = jnp.zeros((step_frames, group, chan), F32)
            out_imag = jnp.zeros((step_frames, group, chan), F32)
            for tap in range(fir):
                window = pl.ds(first + fir - 1 - tap, step_frames)
                part_real = spectra[0, window]
                part_imag = spectra[1, window]
                out_real = out_real + taps[0, tap] * part_real - taps[1, tap] * part_imag
                out_imag = out_imag + taps[0, tap] * part_imag + taps[1, tap] * part_real
            rows = pl.ds(pl.multiple_of(first * group, group), step_frames * group)
            filtered[0, rows, :] = out_real.reshape(step_frames * group, chan)
            filtered[1, rows, :] = out_imag.reshape(step_frames * group, chan)

        for chunk in range(chunks):
            for pair in range(pairs):
                tile = [
                    filtered[part, pl.ds(chunk * CHUNK * group + dish, CHUNK, stride=group), :]
                    for dish in (2 * pair, 2 * pair + 1)
                    for part in range(2)
                ]
                turned[chunk, pair] = jnp.concatenate(tile, axis=0).T

        @pl.loop(0, devices)
        def _(step):
            device = lax.rem(me + step, devices)
            start = pl.multiple_of(device // owners * band_chans, band_chans)
            source = turned.at[:, :, pl.ds(start, band_chans), :]

            @pl.when(device != me)
            def _():
                pltpu.make_async_remote_copy(
                    src_ref=source,
                    dst_ref=panels.at[:, worker],
                    send_sem=sems.at[2],
                    recv_sem=sems.at[3],
                    device_id={"band": device},
                ).start()

            @pl.when(device == me)
            def _():
                pltpu.make_async_copy(source, panels.at[:, worker], sems.at[3]).start()

    pltpu.make_async_copy(panels, panels, sems.at[3]).wait()

    lane_b = lax.broadcasted_iota(jnp.int32, (beams, 4 * CHUNK), 1)
    per_chunk = CHUNK // INTEG
    columns = per_chunk * chunks
    from_lane = lax.broadcasted_iota(jnp.int32, (4 * CHUNK, columns), 0)
    to_column = lax.broadcasted_iota(jnp.int32, (4 * CHUNK, columns), 1)
    in_part = jnp.where(from_lane < CHUNK, from_lane, from_lane - CHUNK)
    flat = panels.reshape(chunks, half * band_chans, 4 * CHUNK)
    for index in range(band_chans):
        power = jnp.zeros((beams, columns), F32)
        lhs = (beams_high[index], beams_low[index])
        for chunk in range(chunks):
            field = flat[chunk, pl.ds(index, half, stride=band_chans), :]
            both = jnp.concatenate([field, pltpu.roll(field, 2 * CHUNK, 1)], axis=0)
            product = dot3(lhs, split(both))
            upper = product[:beams]
            lower = product[beams:]
            crossed = jnp.where(
                lane_b < CHUNK,
                -pltpu.roll(lower, 3 * CHUNK, 1),
                pltpu.roll(lower, CHUNK, 1),
            )
            beam = upper + crossed
            energy = split(beam * beam)
            pick = jnp.logical_and(
                from_lane < 2 * CHUNK, in_part // INTEG + per_chunk * chunk == to_column
            )
            mean = jnp.where(pick, 1.0 / INTEG, 0.0).astype(BF16)
            power = power + (dot(energy[0], mean) + dot(energy[1], mean))
        out_ref[0, index] = power

    @pl.when(active)
    def _():
        sent = stage.at[pl.ds(0, workers - 1)]
        pltpu.make_async_copy(sent, sent, sems.at[0]).wait()
        for _ in range(owners - 1):
            pltpu.make_async_copy(turned, turned, sems.at[2]).wait()
        rest = turned.at[:, :, pl.ds(0, chan - band_chans), :]
        pltpu.make_async_copy(rest, rest, sems.at[2]).wait()

    @pl.when(jnp.logical_not(active))
    def _():
        pltpu.make_async_copy(stage, stage, sems.at[0]).wait()


def body(devices, samples, prototype, dish_filter, beam_weights, dish_order):
    pfb, chan = prototype.shape
    fir, dishes = dish_filter.shape[1:3]
    band_chans, _, _, beams = beam_weights.shape[1:]
    owners = devices // (chan // band_chans)
    slice_frames = samples.shape[2] // chan
    frames = slice_frames * devices
    group = 8 * (-(-dishes // (8 * devices)))
    workers = dishes // group
    chunks = frames // CHUNK
    pairs = group // 2
    dims = (devices, workers, group, slice_frames, frames, owners)
    any_spec = pl.BlockSpec(memory_space=pl.ANY)
    vmem_spec = pl.BlockSpec(memory_space=pltpu.VMEM)
    return pl.pallas_call(
        functools.partial(kernel, dims),
        out_shape=jax.ShapeDtypeStruct((1, band_chans, beams, frames // INTEG), F32),
        in_specs=[vmem_spec, vmem_spec, vmem_spec, any_spec, any_spec, any_spec],
        out_specs=vmem_spec,
        scratch_shapes=[
            pltpu.VMEM((workers, slice_frames, 2, group, chan), F32),
            pltpu.VMEM((pfb - 1 + frames, 2, group, chan), F32),
            pltpu.VMEM((2, fir - 1 + frames, group, chan), F32),
            pltpu.VMEM((2, frames * group, chan), F32),
            pltpu.VMEM((chunks, pairs, chan, 4 * CHUNK), F32),
            pltpu.VMEM((chunks, workers, pairs, band_chans, 4 * CHUNK), F32),
            pltpu.VMEM((2, 2 * chan, 2 * chan), BF16),
            pltpu.VMEM((2, fir, group, chan), F32),
            pltpu.VMEM((band_chans, 2, dishes, beams), F32),
            pltpu.VMEM((band_chans, 2 * beams, dishes), BF16),
            pltpu.VMEM((band_chans, 2 * beams, dishes), BF16),
            pltpu.SemaphoreType.DMA((3,)),
            pltpu.SemaphoreType.DMA((4,)),
        ],
        compiler_params=pltpu.CompilerParams(
            collective_id=0, has_side_effects=True, vmem_limit_bytes=48 * 2**20
        ),
    )(
        samples,
        prototype,
        dish_order.reshape(1, dishes),
        jnp.asarray(fourier_matrix(chan)),
        dish_filter,
        beam_weights,
    )


def solution(mesh):
    placed = (P(None, None, ("grp", "band")), P(), P(), P("band", None, None, None, None), P())
    return jax.shard_map(
        functools.partial(body, mesh.shape["band"]),
        mesh=mesh,
        in_specs=placed,
        out_specs=P(("grp", "band"), None, None, None),
        check_vma=False,
    )
```

```python
import functools
import math

import jax
import jax.numpy as jnp
import ml_dtypes
import numpy as np
from jax import lax
from jax.experimental import pallas as pl
from jax.experimental.pallas import tpu as pltpu
from jax.sharding import PartitionSpec as P

INTEG = 4
CHUNK = 32
SUB = 8
F32 = jnp.float32
BF16 = jnp.bfloat16


def split(value):
    high = value.astype(BF16)
    return high, (value - high.astype(F32)).astype(BF16)


def dot(lhs, rhs):
    return jnp.dot(lhs, rhs, preferred_element_type=F32)


def dot3(lhs, rhs):
    return dot(lhs[0], rhs[0]) + (dot(lhs[0], rhs[1]) + dot(lhs[1], rhs[0]))


def fourier_matrix(length):
    counter = np.arange(length)
    angles = (counter[:, None] * counter[None, :] % length) * (2.0 * math.pi / length)
    cosine = np.cos(angles) / math.sqrt(length)
    sine = np.sin(angles) / math.sqrt(length)
    full = np.block([[cosine, -sine], [sine, cosine]]).astype(np.float32)
    high = full.astype(ml_dtypes.bfloat16)
    low = (full - high.astype(np.float32)).astype(ml_dtypes.bfloat16)
    return np.stack([high, low])


def kernel(
    dims,
    x_hbm,
    proto_hbm,
    order_hbm,
    fourier_hbm,
    taps_hbm,
    weights_hbm,
    out_ref,
    stage,
    voltages,
    spectra,
    filtered,
    turned,
    panels,
    proto_ref,
    order_ref,
    fourier,
    taps,
    weights,
    beams_high,
    beams_low,
    partial,
    load_sems,
    send_sems,
    voltage_sems,
    panel_sems,
):
    devices, workers, group, slice_frames, frames, owners = dims
    pfb = proto_ref.shape[0]
    chan = proto_ref.shape[1]
    fir = taps.shape[1]
    dishes = order_ref.shape[1]
    band_chans, _, _, beams = weights.shape
    halves = group // SUB
    pairs = SUB // 2
    chunks = frames // CHUNK
    rows_half = workers * pairs
    me = lax.axis_index("band")
    worker = (me * workers + devices - 1) // devices
    active = jnp.logical_and(worker < workers, worker * devices // workers == me)
    worker = jnp.minimum(worker, workers - 1)
    dish_start = pl.multiple_of(worker * group, group)

    load_weights = pltpu.make_async_copy(weights_hbm.at[0], weights, load_sems.at[5])
    load_taps = pltpu.make_async_copy(
        taps_hbm.at[:, :, pl.ds(dish_start, group), :], taps, load_sems.at[1]
    )
    load_fourier = pltpu.make_async_copy(fourier_hbm, fourier, load_sems.at[2])

    load_order = pltpu.make_async_copy(order_hbm, order_ref, load_sems.at[3])
    load_proto = pltpu.make_async_copy(proto_hbm, proto_ref, load_sems.at[4])
    for frame in range(slice_frames):
        pltpu.make_async_copy(
            x_hbm.at[:, :, frame * chan : (frame + 1) * chan], stage.at[frame], load_sems.at[0]
        ).start()

    barrier = pltpu.get_barrier_semaphore()

    @pl.loop(1, devices)
    def _(step):
        pl.semaphore_signal(barrier, inc=1, device_id={"band": lax.rem(me + step, devices)})

    load_order.start()
    load_proto.start()
    load_weights.start()
    load_taps.start()
    load_fourier.start()
    pltpu.make_async_copy(stage, stage, load_sems.at[0]).wait()
    pl.semaphore_wait(barrier, devices - 1)

    arrival = pl.ds(pfb - 1 + me * slice_frames, slice_frames)

    for half in range(halves):

        @pl.loop(0, workers)
        def _(step):
            target = lax.rem(worker + step, workers)
            device = target * devices // workers
            start = pl.multiple_of(target * group + half * SUB, SUB)
            outgoing = stage.at[:, :, pl.ds(start, SUB), :]
            landing = voltages.at[half, arrival]

            @pl.when(device != me)
            def _():
                pltpu.make_async_remote_copy(
                    src_ref=outgoing,
                    dst_ref=landing,
                    send_sem=send_sems.at[0],
                    recv_sem=voltage_sems.at[half],
                    device_id={"band": device},
                ).start()

            @pl.when(device == me)
            def _():
                pltpu.make_async_copy(outgoing, landing, voltage_sems.at[half]).start()

    load_order.wait()
    row = lax.broadcasted_iota(jnp.int32, (dishes, dishes), 0)
    dish_of_row = jnp.zeros((dishes, dishes), jnp.int32)
    for block in range(2 * halves):
        rest = row - block * rows_half
        dish = rest // pairs * group + rest % pairs * 2 + block // 2 * SUB + block % 2
        dish_of_row = jnp.where(rest >= 0, dish, dish_of_row)
    chosen = jnp.where(order_ref[...] == dish_of_row, 1.0, 0.0).astype(BF16)
    load_weights.wait()

    @pl.loop(0, band_chans)
    def _(index):
        for part in range(2):
            high, low = split(weights[index, part])
            beams_high[index, part] = dot(chosen, high).astype(BF16)
            beams_low[index, part] = dot(chosen, low).astype(BF16)

    load_proto.wait()
    load_taps.wait()
    load_fourier.wait()

    @pl.when(active)
    def _():
        spectra[:, 0 : fir - 1] = jnp.zeros((2, fir - 1, SUB, chan), F32)
        for half in range(halves):
            voltages[half, 0 : pfb - 1] = jnp.zeros((pfb - 1, 2, SUB, chan), F32)
        step_frames = 16
        for half in range(halves):
            landed = voltages.at[half, pl.ds(pfb - 1, frames)]
            pltpu.make_async_copy(landed, landed, voltage_sems.at[half]).wait()

            @pl.loop(0, frames // step_frames)
            def _(step):
                first = step * step_frames
                pieces = []
                for part in range(2):
                    total = jnp.zeros((step_frames, SUB, chan), F32)
                    for tap in range(pfb):
                        total = total + proto_ref[tap : tap + 1, :] * voltages[
                            half, pl.ds(first + pfb - 1 - tap, step_frames), part
                        ]
                    pieces.append(total.reshape(step_frames * SUB, chan))
                lhs = split(jnp.concatenate(pieces, axis=1))
                result = dot3(lhs, (fourier[0], fourier[1]))
                for part in range(2):
                    spectra[part, pl.ds(first + fir - 1, step_frames)] = result[
                        :, part * chan : (part + 1) * chan
                    ].reshape(step_frames, SUB, chan)

            @pl.loop(0, frames // step_frames)
            def _(step):
                first = step * step_frames
                out_real = jnp.zeros((step_frames, SUB, chan), F32)
                out_imag = jnp.zeros((step_frames, SUB, chan), F32)
                for tap in range(fir):
                    window = pl.ds(first + fir - 1 - tap, step_frames)
                    part_real = spectra[0, window]
                    part_imag = spectra[1, window]
                    tap_real = taps[0, tap, half * SUB : (half + 1) * SUB]
                    tap_imag = taps[1, tap, half * SUB : (half + 1) * SUB]
                    out_real = out_real + tap_real * part_real - tap_imag * part_imag
                    out_imag = out_imag + tap_real * part_imag + tap_imag * part_real
                rows = pl.ds(pl.multiple_of(first * SUB, SUB), step_frames * SUB)
                filtered[0, rows, :] = out_real.reshape(step_frames * SUB, chan)
                filtered[1, rows, :] = out_imag.reshape(step_frames * SUB, chan)

            for chunk in range(chunks):
                for pair in range(pairs):
                    tile = [
                        filtered[part, pl.ds(chunk * CHUNK * SUB + dish, CHUNK, stride=SUB), :]
                        for dish in (2 * pair, 2 * pair + 1)
                        for part in range(2)
                    ]
                    turned[half, chunk, pair] = jnp.concatenate(tile, axis=0).T

            @pl.loop(0, devices)
            def _(step):
                device = lax.rem(me + step, devices)
                start = pl.multiple_of(device // owners * band_chans, band_chans)
                source = turned.at[half, :, :, pl.ds(start, band_chans), :]
                landing = panels.at[half, :, worker]

                @pl.when(device != me)
                def _():
                    pltpu.make_async_remote_copy(
                        src_ref=source,
                        dst_ref=landing,
                        send_sem=send_sems.at[1],
                        recv_sem=panel_sems.at[half],
                        device_id={"band": device},
                    ).start()

                @pl.when(device == me)
                def _():
                    pltpu.make_async_copy(source, landing, panel_sems.at[half]).start()

    per_chunk = CHUNK // INTEG
    from_frame = lax.broadcasted_iota(jnp.int32, (per_chunk, CHUNK), 1)
    to_sample = lax.broadcasted_iota(jnp.int32, (per_chunk, CHUNK), 0)
    mean = jnp.where(from_frame // INTEG == to_sample, 1.0 / INTEG, 0.0).astype(BF16)
    flat = panels.reshape(halves, chunks, rows_half * band_chans, 4 * CHUNK)
    for half in range(halves):
        pltpu.make_async_copy(panels.at[half], panels.at[half], panel_sems.at[half]).wait()
        depth = slice(2 * half * rows_half, 2 * (half + 1) * rows_half)
        for index in range(band_chans):
            for chunk in range(chunks):
                field = flat[half, chunk, pl.ds(index, rows_half, stride=band_chans), :]
                both = jnp.concatenate([field, pltpu.roll(field, 2 * CHUNK, 1)], axis=0)
                high, low = split(both.T[: 2 * CHUNK])
                stacked = jnp.concatenate([high, low], axis=0)
                products = []
                for part in range(2):
                    wide = dot(stacked, beams_high[index, part, depth, :])
                    total = wide[: 2 * CHUNK] + (
                        wide[2 * CHUNK :] + dot(high, beams_low[index, part, depth, :])
                    )
                    if half > 0:
                        total = total + partial[index, chunk, part]
                    if half < halves - 1:
                        partial[index, chunk, part] = total
                    products.append(total)
                if half == halves - 1:
                    real = products[0][:CHUNK] - products[1][CHUNK:]
                    imag = products[0][CHUNK:] + products[1][:CHUNK]
                    energy = split(real * real + imag * imag)
                    out_ref[0, index, chunk * per_chunk : (chunk + 1) * per_chunk, :] = dot(
                        mean, energy[0]
                    ) + dot(mean, energy[1])

    @pl.when(active)
    def _():
        sent = stage.at[:, :, pl.ds(0, dishes - group), :]
        pltpu.make_async_copy(sent, sent, send_sems.at[0]).wait()
        for _ in range(owners - 1):
            pltpu.make_async_copy(turned, turned, send_sems.at[1]).wait()
        rest = turned.at[:, :, :, pl.ds(0, chan - band_chans), :]
        pltpu.make_async_copy(rest, rest, send_sems.at[1]).wait()

    @pl.when(jnp.logical_not(active))
    def _():
        pltpu.make_async_copy(stage, stage, send_sems.at[0]).wait()


def body(devices, samples, prototype, dish_filter, beam_weights, dish_order):
    pfb, chan = prototype.shape
    fir, dishes = dish_filter.shape[1:3]
    band_chans, _, _, beams = beam_weights.shape[1:]
    owners = devices // (chan // band_chans)
    slice_frames = samples.shape[2] // chan
    frames = slice_frames * devices
    group = SUB * (-(-dishes // (SUB * devices)))
    workers = dishes // group
    chunks = frames // CHUNK
    halves = group // SUB
    pairs = SUB // 2
    dims = (devices, workers, group, slice_frames, frames, owners)
    hbm_spec = pl.BlockSpec(memory_space=pltpu.HBM)
    vmem_spec = pl.BlockSpec(memory_space=pltpu.VMEM)
    power = pl.pallas_call(
        functools.partial(kernel, dims),
        out_shape=jax.ShapeDtypeStruct((1, band_chans, frames // INTEG, beams), F32),
        in_specs=[hbm_spec] * 6,
        out_specs=vmem_spec,
        scratch_shapes=[
            pltpu.VMEM((slice_frames, 2, dishes, chan), F32),
            pltpu.VMEM((halves, pfb - 1 + frames, 2, SUB, chan), F32),
            pltpu.VMEM((2, fir - 1 + frames, SUB, chan), F32),
            pltpu.VMEM((2, frames * SUB, chan), F32),
            pltpu.VMEM((halves, chunks, pairs, chan, 4 * CHUNK), F32),
            pltpu.VMEM((halves, chunks, workers, pairs, band_chans, 4 * CHUNK), F32),
            pltpu.VMEM((pfb, chan), F32),
            pltpu.VMEM((1, dishes), jnp.int32),
            pltpu.VMEM((2, 2 * chan, 2 * chan), BF16),
            pltpu.VMEM((2, fir, group, chan), F32),
            pltpu.VMEM((band_chans, 2, dishes, beams), F32),
            pltpu.VMEM((band_chans, 2, dishes, beams), BF16),
            pltpu.VMEM((band_chans, 2, dishes, beams), BF16),
            pltpu.VMEM((band_chans, chunks, 2, 2 * CHUNK, beams), F32),
            pltpu.SemaphoreType.DMA((6,)),
            pltpu.SemaphoreType.DMA((2,)),
            pltpu.SemaphoreType.DMA((halves,)),
            pltpu.SemaphoreType.DMA((halves,)),
        ],
        compiler_params=pltpu.CompilerParams(
            collective_id=0, has_side_effects=True, vmem_limit_bytes=60 * 2**20
        ),
    )(
        samples,
        prototype,
        dish_order.reshape(1, dishes),
        jnp.asarray(fourier_matrix(chan)),
        dish_filter,
        beam_weights,
    )
    return jnp.swapaxes(power, 2, 3)


def solution(mesh):
    placed = (P(None, None, ("grp", "band")), P(), P(), P("band", None, None, None, None), P())
    return jax.shard_map(
        functools.partial(body, mesh.shape["band"]),
        mesh=mesh,
        in_specs=placed,
        out_specs=P(("grp", "band"), None, None, None),
        check_vma=False,
    )
```

```python
import functools
import math

import jax
import jax.numpy as jnp
import ml_dtypes
import numpy as np
from jax import lax
from jax.experimental import pallas as pl
from jax.experimental.pallas import tpu as pltpu
from jax.sharding import PartitionSpec as P

INTEG = 4
CHUNK = 32
SUB = 8
F32 = jnp.float32
BF16 = jnp.bfloat16


def split(value):
    high = value.astype(BF16)
    return high, (value - high.astype(F32)).astype(BF16)


def dot(lhs, rhs):
    return jnp.dot(lhs, rhs, preferred_element_type=F32)


def dot3(lhs, rhs):
    return dot(lhs[0], rhs[0]) + (dot(lhs[0], rhs[1]) + dot(lhs[1], rhs[0]))


def fourier_matrix(length):
    counter = np.arange(length)
    angles = (counter[:, None] * counter[None, :] % length) * (2.0 * math.pi / length)
    cosine = np.cos(angles) / math.sqrt(length)
    sine = np.sin(angles) / math.sqrt(length)
    full = np.block([[cosine, -sine], [sine, cosine]]).astype(np.float32)
    high = full.astype(ml_dtypes.bfloat16)
    low = (full - high.astype(np.float32)).astype(ml_dtypes.bfloat16)
    return np.stack([high, low])


def kernel(
    dims,
    x_hbm,
    proto_hbm,
    order_hbm,
    fourier_hbm,
    taps_hbm,
    weights_hbm,
    out_ref,
    stage,
    voltages,
    spectra,
    filtered,
    turned,
    panels,
    proto_ref,
    order_ref,
    fourier,
    taps,
    weights,
    beams_high,
    beams_low,
    partial,
    load_sems,
    send_sems,
    voltage_sems,
    panel_sems,
):
    devices, workers, group, slice_frames, frames, owners = dims
    pfb = proto_ref.shape[0]
    chan = proto_ref.shape[1]
    fir = taps.shape[1]
    dishes = order_ref.shape[1]
    band_chans, _, _, beams = weights.shape
    halves = group // SUB
    pairs = SUB // 2
    chunks = frames // CHUNK
    rows_half = workers * pairs
    me = lax.axis_index("band")
    worker = (me * workers + devices - 1) // devices
    active = jnp.logical_and(worker < workers, worker * devices // workers == me)
    worker = jnp.minimum(worker, workers - 1)
    dish_start = pl.multiple_of(worker * group, group)

    load_weights = pltpu.make_async_copy(weights_hbm.at[0], weights, load_sems.at[5])
    load_taps = pltpu.make_async_copy(
        taps_hbm.at[:, :, pl.ds(dish_start, group), :], taps, load_sems.at[1]
    )
    load_fourier = pltpu.make_async_copy(fourier_hbm, fourier, load_sems.at[2])

    load_order = pltpu.make_async_copy(order_hbm, order_ref, load_sems.at[3])
    load_proto = pltpu.make_async_copy(proto_hbm, proto_ref, load_sems.at[4])
    for frame in range(slice_frames):
        pltpu.make_async_copy(
            x_hbm.at[:, :, frame * chan : (frame + 1) * chan], stage.at[frame], load_sems.at[0]
        ).start()

    barrier = pltpu.get_barrier_semaphore()

    @pl.loop(1, devices)
    def _(step):
        pl.semaphore_signal(barrier, inc=1, device_id={"band": lax.rem(me + step, devices)})

    load_order.start()
    load_proto.start()
    load_weights.start()
    load_taps.start()
    load_fourier.start()
    pltpu.make_async_copy(stage, stage, load_sems.at[0]).wait()
    pl.semaphore_wait(barrier, devices - 1)

    arrival = pl.ds(pfb - 1 + me * slice_frames, slice_frames)

    for half in range(halves):

        @pl.loop(0, workers)
        def _(step):
            target = lax.rem(worker + step, workers)
            device = target * devices // workers
            start = pl.multiple_of(target * group + half * SUB, SUB)
            outgoing = stage.at[:, :, pl.ds(start, SUB), :]
            landing = voltages.at[half, arrival]

            @pl.when(device != me)
            def _():
                pltpu.make_async_remote_copy(
                    src_ref=outgoing,
                    dst_ref=landing,
                    send_sem=send_sems.at[0],
                    recv_sem=voltage_sems.at[half],
                    device_id={"band": device},
                ).start()

            @pl.when(device == me)
            def _():
                pltpu.make_async_copy(outgoing, landing, voltage_sems.at[half]).start()

    load_proto.wait()
    load_taps.wait()
    load_fourier.wait()

    step_frames = 16

    def prepare():
        load_order.wait()
        row = lax.broadcasted_iota(jnp.int32, (dishes, dishes), 0)
        dish_of_row = jnp.zeros((dishes, dishes), jnp.int32)
        for block in range(2 * halves):
            rest = row - block * rows_half
            dish = rest // pairs * group + rest % pairs * 2 + block // 2 * SUB + block % 2
            dish_of_row = jnp.where(rest >= 0, dish, dish_of_row)
        chosen = jnp.where(order_ref[...] == dish_of_row, 1.0, 0.0).astype(BF16)
        load_weights.wait()

        @pl.loop(0, band_chans)
        def _(index):
            for part in range(2):
                high, low = split(weights[index, part])
                beams_high[index, part] = dot(chosen, high).astype(BF16)
                beams_low[index, part] = dot(chosen, low).astype(BF16)

    @pl.when(active)
    def _():
        spectra[:, 0 : fir - 1] = jnp.zeros((2, fir - 1, SUB, chan), F32)
        for half in range(halves):
            voltages[half, 0 : pfb - 1] = jnp.zeros((pfb - 1, 2, SUB, chan), F32)

    for half in range(halves):

        @pl.when(active)
        def _():
            landed = voltages.at[half, pl.ds(pfb - 1, frames)]
            pltpu.make_async_copy(landed, landed, voltage_sems.at[half]).wait()

            @pl.loop(0, frames // step_frames)
            def _(step):
                first = step * step_frames
                pieces = []
                for part in range(2):
                    total = jnp.zeros((step_frames, SUB, chan), F32)
                    for tap in range(pfb):
                        total = total + proto_ref[tap : tap + 1, :] * voltages[
                            half, pl.ds(first + pfb - 1 - tap, step_frames), part
                        ]
                    pieces.append(total.reshape(step_frames * SUB, chan))
                lhs = split(jnp.concatenate(pieces, axis=1))
                result = dot3(lhs, (fourier[0], fourier[1]))
                for part in range(2):
                    spectra[part, pl.ds(first + fir - 1, step_frames)] = result[
                        :, part * chan : (part + 1) * chan
                    ].reshape(step_frames, SUB, chan)

            @pl.loop(0, frames // step_frames)
            def _(step):
                first = step * step_frames
                out_real = jnp.zeros((step_frames, SUB, chan), F32)
                out_imag = jnp.zeros((step_frames, SUB, chan), F32)
                for tap in range(fir):
                    window = pl.ds(first + fir - 1 - tap, step_frames)
                    part_real = spectra[0, window]
                    part_imag = spectra[1, window]
                    tap_real = taps[0, tap, half * SUB : (half + 1) * SUB]
                    tap_imag = taps[1, tap, half * SUB : (half + 1) * SUB]
                    out_real = out_real + tap_real * part_real - tap_imag * part_imag
                    out_imag = out_imag + tap_real * part_imag + tap_imag * part_real
                rows = pl.ds(pl.multiple_of(first * SUB, SUB), step_frames * SUB)
                filtered[0, rows, :] = out_real.reshape(step_frames * SUB, chan)
                filtered[1, rows, :] = out_imag.reshape(step_frames * SUB, chan)

            for chunk in range(chunks):
                for pair in range(pairs):
                    tile = [
                        filtered[part, pl.ds(chunk * CHUNK * SUB + dish, CHUNK, stride=SUB), :]
                        for dish in (2 * pair, 2 * pair + 1)
                        for part in range(2)
                    ]
                    turned[half, chunk, pair] = jnp.concatenate(tile, axis=0).T

            @pl.loop(0, devices)
            def _(step):
                device = lax.rem(me + step, devices)
                start = pl.multiple_of(device // owners * band_chans, band_chans)
                source = turned.at[half, :, :, pl.ds(start, band_chans), :]
                landing = panels.at[half, :, worker]

                @pl.when(device != me)
                def _():
                    pltpu.make_async_remote_copy(
                        src_ref=source,
                        dst_ref=landing,
                        send_sem=send_sems.at[1],
                        recv_sem=panel_sems.at[half],
                        device_id={"band": device},
                    ).start()

                @pl.when(device == me)
                def _():
                    pltpu.make_async_copy(source, landing, panel_sems.at[half]).start()

        if half == 0:
            prepare()

    per_chunk = CHUNK // INTEG
    from_frame = lax.broadcasted_iota(jnp.int32, (per_chunk, CHUNK), 1)
    to_sample = lax.broadcasted_iota(jnp.int32, (per_chunk, CHUNK), 0)
    mean = jnp.where(from_frame // INTEG == to_sample, 1.0 / INTEG, 0.0).astype(BF16)
    flat = panels.reshape(halves, chunks, rows_half * band_chans, 4 * CHUNK)
    for half in range(halves):
        pltpu.make_async_copy(panels.at[half], panels.at[half], panel_sems.at[half]).wait()
        depth = slice(2 * half * rows_half, 2 * (half + 1) * rows_half)
        for index in range(band_chans):
            for chunk in range(chunks):
                field = flat[half, chunk, pl.ds(index, rows_half, stride=band_chans), :]
                both = jnp.concatenate([field, pltpu.roll(field, 2 * CHUNK, 1)], axis=0)
                high, low = split(both.T[: 2 * CHUNK])
                stacked = jnp.concatenate([high, low], axis=0)
                products = []
                for part in range(2):
                    wide = dot(stacked, beams_high[index, part, depth, :])
                    total = wide[: 2 * CHUNK] + (
                        wide[2 * CHUNK :] + dot(high, beams_low[index, part, depth, :])
                    )
                    if half > 0:
                        total = total + partial[index, chunk, part]
                    if half < halves - 1:
                        partial[index, chunk, part] = total
                    products.append(total)
                if half == halves - 1:
                    real = products[0][:CHUNK] - products[1][CHUNK:]
                    imag = products[0][CHUNK:] + products[1][:CHUNK]
                    energy = split(real * real + imag * imag)
                    out_ref[0, index, chunk * per_chunk : (chunk + 1) * per_chunk, :] = dot(
                        mean, energy[0]
                    ) + dot(mean, energy[1])

    @pl.when(active)
    def _():
        sent = stage.at[:, :, pl.ds(0, dishes - group), :]
        pltpu.make_async_copy(sent, sent, send_sems.at[0]).wait()
        for _ in range(owners - 1):
            pltpu.make_async_copy(turned, turned, send_sems.at[1]).wait()
        rest = turned.at[:, :, :, pl.ds(0, chan - band_chans), :]
        pltpu.make_async_copy(rest, rest, send_sems.at[1]).wait()

    @pl.when(jnp.logical_not(active))
    def _():
        pltpu.make_async_copy(stage, stage, send_sems.at[0]).wait()


def body(devices, samples, prototype, dish_filter, beam_weights, dish_order):
    pfb, chan = prototype.shape
    fir, dishes = dish_filter.shape[1:3]
    band_chans, _, _, beams = beam_weights.shape[1:]
    owners = devices // (chan // band_chans)
    slice_frames = samples.shape[2] // chan
    frames = slice_frames * devices
    group = SUB * (-(-dishes // (SUB * devices)))
    workers = dishes // group
    chunks = frames // CHUNK
    halves = group // SUB
    pairs = SUB // 2
    dims = (devices, workers, group, slice_frames, frames, owners)
    hbm_spec = pl.BlockSpec(memory_space=pltpu.HBM)
    vmem_spec = pl.BlockSpec(memory_space=pltpu.VMEM)
    power = pl.pallas_call(
        functools.partial(kernel, dims),
        out_shape=jax.ShapeDtypeStruct((1, band_chans, frames // INTEG, beams), F32),
        in_specs=[hbm_spec] * 6,
        out_specs=vmem_spec,
        scratch_shapes=[
            pltpu.VMEM((slice_frames, 2, dishes, chan), F32),
            pltpu.VMEM((halves, pfb - 1 + frames, 2, SUB, chan), F32),
            pltpu.VMEM((2, fir - 1 + frames, SUB, chan), F32),
            pltpu.VMEM((2, frames * SUB, chan), F32),
            pltpu.VMEM((halves, chunks, pairs, chan, 4 * CHUNK), F32),
            pltpu.VMEM((halves, chunks, workers, pairs, band_chans, 4 * CHUNK), F32),
            pltpu.VMEM((pfb, chan), F32),
            pltpu.VMEM((1, dishes), jnp.int32),
            pltpu.VMEM((2, 2 * chan, 2 * chan), BF16),
            pltpu.VMEM((2, fir, group, chan), F32),
            pltpu.VMEM((band_chans, 2, dishes, beams), F32),
            pltpu.VMEM((band_chans, 2, dishes, beams), BF16),
            pltpu.VMEM((band_chans, 2, dishes, beams), BF16),
            pltpu.VMEM((band_chans, chunks, 2, 2 * CHUNK, beams), F32),
            pltpu.SemaphoreType.DMA((6,)),
            pltpu.SemaphoreType.DMA((2,)),
            pltpu.SemaphoreType.DMA((halves,)),
            pltpu.SemaphoreType.DMA((halves,)),
        ],
        compiler_params=pltpu.CompilerParams(
            collective_id=0, has_side_effects=True, vmem_limit_bytes=60 * 2**20
        ),
    )(
        samples,
        prototype,
        dish_order.reshape(1, dishes),
        jnp.asarray(fourier_matrix(chan)),
        dish_filter,
        beam_weights,
    )
    return jnp.swapaxes(power, 2, 3)


def solution(mesh):
    placed = (P(None, None, ("grp", "band")), P(), P(), P("band", None, None, None, None), P())
    return jax.shard_map(
        functools.partial(body, mesh.shape["band"]),
        mesh=mesh,
        in_specs=placed,
        out_specs=P(("grp", "band"), None, None, None),
        check_vma=False,
    )
```
